32 devices in a mesh: dp: 16 (over z, y, x), sub: 2 (over core).
Axes of the slice: x: 2, y: 2, z: 4, core: 2. Of those that a mesh axis runs over, the one named last changes fastest.
Arguments:
- points: bfloat16 [16384, 256], P(('dp', 'sub'))
- candidates: int32 [4, 768], replicated, may hold values from 0 to 16383, as said below
- owner_slot: int32 [3072], replicated, may hold values from 0 to 3071, each once
Outputs:
- centroids: float32 [3072, 256], P(('dp', 'sub'))
- masses: float32 [3072], P(('dp', 'sub'))
- min_dist: float32 [16384], P(('dp', 'sub'))
The draws below stay inside these ranges and needn't reach their ends.
Inputs may be any that keep to these rules, and one draw needn't show every extreme that they name: In each round the candidates are distinct rows; no device's block of 512 rows holds more than 96 candidates of one round, and in each round some device's block holds exactly 96.
All inputs are finite; a program needn't handle non-finite values.
Results may differ from the reference program's by a relative error of at most 0.00055.
Values may be sent and summed in bfloat16 or wider, within the bound.
No kernel may reach another device: no remote copies, remote signals or barrier semaphores. Data moves between devices by JAX's collectives and lax.ppermute only.
A program may use at most 64 MiB of HBM per device.

```python
import jax
import jax.numpy as jnp
from jax import lax

DIM = 256
CAND = 768
ROUNDS = 4
ROWS_DEV = 512
NPTS = 16384
TOTAL = 3072
MOST = 96
CLUSTER = 128


def draw_points(key, part):
    key_center, key_noise = jax.random.split(key, 2)
    groups = NPTS // CLUSTER
    centers = jax.random.normal(key_center, (groups, DIM), jnp.float32) * DIM ** (-0.5)
    noise = jax.random.normal(key_noise, (NPTS, DIM), jnp.float32) * 0.5 * DIM ** (-0.5)
    values = jnp.repeat(centers, CLUSTER, axis=0) + noise
    return values.astype(jnp.bfloat16)


def draw_candidates(key, part):
    device_count = NPTS // ROWS_DEV
    span = ROWS_DEV // MOST
    rounds_out = []
    for which_round in range(ROUNDS):
        round_key = jax.random.fold_in(key, which_round + 17)
        key_perm, key_row, key_order = jax.random.split(round_key, 3)
        device_perm = jax.random.permutation(key_perm, device_count).astype(jnp.int32)
        positions = jnp.arange(CAND, dtype=jnp.int32)
        heavy = positions < MOST
        others = positions - MOST
        owner_pos = jnp.where(heavy, 0, 1 + others % (device_count - 1))
        slot_no = jnp.where(heavy, positions, others // (device_count - 1))
        owner_dev = device_perm[owner_pos]
        offset = jax.random.randint(key_row, (CAND,), 0, span, jnp.int32)
        row_index = owner_dev * ROWS_DEV + slot_no * span + offset
        order = jax.random.permutation(key_order, CAND)
        rounds_out.append(row_index[order].astype(jnp.int32))
    return jnp.stack(rounds_out, axis=0)


def setup_inputs(seed: int = 0) -> dict:
    arg_keys = jax.random.split(jax.random.key(seed), 4)
    points = draw_points(jax.random.fold_in(arg_keys[3], 71), 0)
    candidates = draw_candidates(jax.random.fold_in(arg_keys[3], 71), 0)
    owner_slot = jax.random.permutation(arg_keys[2], TOTAL).astype(jnp.int32)
    return dict(points=points, candidates=candidates, owner_slot=owner_slot)


def reference(points, candidates, owner_slot):
    chosen = points[candidates.reshape(-1)]
    cand_norm = jnp.sum(chosen.astype(jnp.float32) ** 2, axis=1)
    block_rows = min(4096, NPTS)
    blocks = points.reshape(NPTS // block_rows, block_rows, DIM)

    def one_block(carry, piece):
        sums_acc, mass_acc = carry
        point_norm = jnp.sum(piece.astype(jnp.float32) ** 2, axis=1)
        dots = lax.dot_general(piece, chosen, (((1,), (1,)), ((), ())), preferred_element_type=jnp.float32)
        dist = point_norm[:, None] + cand_norm[None, :] - 2.0 * dots
        nearest = jnp.min(dist, axis=1)
        kernel = jnp.exp(-dist / 0.25).astype(jnp.bfloat16)
        sums_acc = sums_acc + lax.dot_general(kernel, piece, (((0,), (0,)), ((), ())), preferred_element_type=jnp.float32)
        mass_acc = mass_acc + jnp.sum(kernel.astype(jnp.float32), axis=0)
        return (sums_acc, mass_acc), nearest

    start = (jnp.zeros((TOTAL, DIM), jnp.float32), jnp.zeros((TOTAL,), jnp.float32))
    (sums, mass), nearest = lax.scan(one_block, start, blocks)
    centroids = jnp.zeros((TOTAL, DIM), jnp.float32).at[owner_slot].set(sums / mass[:, None])
    masses = jnp.zeros((TOTAL,), jnp.float32).at[owner_slot].set(mass)
    return centroids, masses, nearest.reshape(NPTS)
```

```python
import functools

import jax
import jax.numpy as jnp
from jax import lax
from jax.experimental import pallas as pl
from jax.experimental.pallas import tpu as pltpu
from jax.sharding import PartitionSpec as P

AXES = ("dp", "sub")
FAR = 3e38
LANES = 128


def pick_rows(round_rows, points, my_device):
    row_count = points.shape[0]
    flat_rows = round_rows.reshape(-1)
    owner_dev = flat_rows // row_count
    local_row = flat_rows % row_count
    mine = owner_dev == my_device
    picked = jnp.where(
        mine[:, None], points[local_row].astype(jnp.float32), jnp.zeros((), jnp.float32)
    )
    return lax.psum(picked, AXES).astype(jnp.bfloat16)


def any_mesh(points, candidates, owner_slot):
    cand = jnp.zeros((owner_slot.shape[0],), jnp.int32).at[owner_slot].set(candidates.reshape(-1))
    chosen = pick_rows(cand, points, lax.axis_index(AXES))
    point_norm = jnp.sum(points.astype(jnp.float32) ** 2, axis=1)
    cand_norm = jnp.sum(chosen.astype(jnp.float32) ** 2, axis=1)
    dots = lax.dot_general(
        points, chosen, (((1,), (1,)), ((), ())), preferred_element_type=jnp.float32
    )
    dist = point_norm[:, None] + cand_norm[None, :] - 2.0 * dots
    nearest = jnp.min(dist, axis=1)
    kernel = jnp.exp(-dist / 0.25).astype(jnp.bfloat16)
    sums = lax.dot_general(
        kernel, points, (((0,), (0,)), ((), ())), preferred_element_type=jnp.float32
    )
    mass = jnp.sum(kernel.astype(jnp.float32), axis=0)
    summed = lax.psum_scatter(sums, AXES, scatter_dimension=0, tiled=True)
    masses = lax.psum_scatter(mass, AXES, scatter_dimension=0, tiled=True)
    return summed / masses[:, None], masses, nearest


def send(x, chips, target):
    pairs = [(d * 2 + c, target(d, c)) for d in range(chips) for c in range(2)]
    return lax.ppermute(x, AXES, pairs)


def scan_kernel(first, counts, base_ref, cand_ref, bias_ref, own_ref, sib_ref, *refs):
    n = len(counts)
    block_refs, (sel_in, near_in), (sel_out, near_out) = refs[:n], refs[n : n + 2], refs[n + 2 :]
    rows, dim = own_ref.shape
    wanted = cand_ref.shape[0]
    sel = sel_in[...]
    nears = [near_in[:, :rows], near_in[:, rows:]]
    lane = lax.broadcasted_iota(jnp.int32, (LANES, LANES), 1)
    spot = lax.broadcasted_iota(jnp.int32, (wanted, rows), 1)
    k = first
    for ref, count in zip(block_refs, counts):
        for j in range(count):
            base = base_ref[k]
            k += 1
            block = ref[j * rows : (j + 1) * rows, :]
            hot = (spot + base == cand_ref[...]).astype(jnp.bfloat16)
            sel += jnp.dot(hot, block, preferred_element_type=jnp.float32)
            cols = []
            for i in range(rows // LANES):
                piece = block[i * LANES : (i + 1) * LANES, :].astype(jnp.float32)
                square = piece * piece
                folded = jnp.where(lane == base // LANES + i, bias_ref[...], 0.0)
                for w in range(dim // LANES):
                    folded += square[:, w * LANES : (w + 1) * LANES]
                cols.append(jnp.sum(folded, axis=1, keepdims=True))
            col = jnp.concatenate(cols, axis=0)
            twice = block * jnp.bfloat16(-2.0)
            for h, mine in enumerate((own_ref, sib_ref)):
                dots = lax.dot_general(
                    twice, mine[...], (((1,), (1,)), ((), ())), preferred_element_type=jnp.float32
                )
                part = jnp.min((dots + col).reshape(rows // 8, 8, rows), axis=0)
                nears[h] = jnp.minimum(nears[h], part)
    sel_out[...] = sel
    near_out[:, :rows] = nears[0]
    near_out[:, rows:] = nears[1]


def sum_kernel(counts, sel_ref, got_ref, near_ref, *refs):
    n = len(counts)
    block_refs, (mine_ref, theirs_ref) = refs[:n], refs[n:]
    wanted, dim = sel_ref.shape
    half = wanted // 2
    rows = near_ref.shape[1] // 2
    got = got_ref[...].astype(jnp.float32)
    chosen32 = sel_ref[...] + jnp.concatenate([got[half:], got[:half]], axis=0)
    chosen = chosen32.astype(jnp.bfloat16)
    square = chosen32 * chosen32
    high = square.astype(jnp.bfloat16)
    low = (square - high.astype(jnp.float32)).astype(jnp.bfloat16)
    ones = jnp.ones((8, dim), jnp.bfloat16)
    last = (((1,), (1,)), ((), ()))
    cand_norm = lax.dot_general(ones, high, last, preferred_element_type=jnp.float32)
    cand_norm += lax.dot_general(ones, low, last, preferred_element_type=jnp.float32)
    cand_norm = cand_norm[:1]
    sums = jnp.zeros((wanted, dim), jnp.float32)
    mass = jnp.zeros((8, wanted), jnp.float32)
    for ref, count in zip(block_refs, counts):
        for j in range(count):
            block = ref[j * rows : (j + 1) * rows, :]
            wide = block.astype(jnp.float32)
            norm = jnp.sum(wide * wide, axis=1, keepdims=True)
            dots = lax.dot_general(block, chosen, last, preferred_element_type=jnp.float32)
            dist = (norm + cand_norm) - 2.0 * dots
            kern = jnp.exp(dist * -4.0).astype(jnp.bfloat16)
            mass += jnp.sum(kern.astype(jnp.float32).reshape(rows // 8, 8, wanted), axis=0)
            sums += lax.dot_general(
                kern, block, (((0,), (0,)), ((), ())), preferred_element_type=jnp.float32
            )
    mass = jnp.sum(mass, axis=0, keepdims=True)
    near = jnp.min(near_ref[...], axis=0, keepdims=True)
    for h, ref in enumerate((mine_ref, theirs_ref)):
        ref[:half, :] = sums[h * half : (h + 1) * half]
        pad = jnp.zeros((1, dim - half), jnp.float32)
        ref[half : half + 1, :] = jnp.concatenate([mass[:, h * half : (h + 1) * half], pad], axis=1)
        for w in range(rows // dim):
            ref[half + 1 + w : half + 2 + w, :] = near[:, h * rows + w * dim : h * rows + (w + 1) * dim]
        tail = ref.shape[0] - (half + 1 + rows // dim)
        if tail:
            ref[half + 1 + rows // dim :, :] = jnp.zeros((tail, dim), jnp.float32)


def gathered(chips, points, candidates, owner_slot):
    rows, dim = points.shape
    total = owner_slot.shape[0]
    half = total // (2 * chips)
    layers = chips // 4
    d = lax.axis_index("dp")
    c = lax.axis_index("sub")
    near_bit = jnp.where(c == 0, 1, 2)
    far_bit = 3 - near_bit

    other = functools.partial(send, chips=chips, target=lambda d, c: d * 2 + 1 - c)
    first_hop = functools.partial(
        send, chips=chips, target=lambda d, c: (d ^ (1 if c == 0 else 2)) * 2 + c
    )
    second_hop = functools.partial(
        send, chips=chips, target=lambda d, c: (d ^ (2 if c == 0 else 1)) * 2 + c
    )

    sib = other(points)
    along = [points]
    for m in range(1, layers):
        along.append(send(points, chips, lambda d, c, m=m: (d ^ (4 * m)) * 2 + c))
    groups = []
    origins = []
    for m, block in enumerate(along):
        hop = first_hop(block)
        pair = second_hop(jnp.concatenate([block, hop], axis=0))
        groups.append((block, hop, pair))
        start = d ^ (4 * m)
        origins += [start, start ^ near_bit, start ^ far_bit, start ^ 3]
    base = (jnp.stack(origins) * 2 + c).astype(jnp.int32) * rows

    flat = candidates.reshape(-1)
    order = jnp.arange(2 * half, dtype=jnp.int32)
    slot = jnp.where(order < half, (2 * d + c) * half + order, (2 * d + 1 - c) * half + order - half)
    cand = jnp.sum(
        jnp.where(owner_slot[None, :] == slot[:, None], flat[None, :], 0), axis=1, keepdims=True
    )
    span = 2 * chips * rows // LANES
    low = (flat[None, :] % LANES == jnp.arange(LANES, dtype=jnp.int32)[:, None]).astype(jnp.bfloat16)
    high = (flat[None, :] // LANES == jnp.arange(span, dtype=jnp.int32)[:, None]).astype(jnp.bfloat16)
    hits = lax.dot_general(low, high, (((1,), (1,)), ((), ())), preferred_element_type=jnp.float32)
    bias = jnp.where(hits > 0, 0.0, FAR).astype(jnp.float32)

    smem = pl.BlockSpec(memory_space=pltpu.SMEM)
    vmem = pl.BlockSpec(memory_space=pltpu.VMEM)
    sel = jnp.zeros((2 * half, dim), jnp.float32)
    near = jnp.full((8, 2 * rows), FAR, jnp.float32)
    first = 0
    calls = []
    for g, (block, hop, pair) in enumerate(groups):
        if g == layers - 1:
            calls += [((block, hop), (1, 1)), ((pair,), (2,))]
        else:
            calls += [((block, hop, pair), (1, 1, 2))]
    for blocks, counts in calls:
        work = sum(counts) * rows
        sel, near = pl.pallas_call(
            functools.partial(scan_kernel, first, counts),
            out_shape=(
                jax.ShapeDtypeStruct(sel.shape, jnp.float32),
                jax.ShapeDtypeStruct(near.shape, jnp.float32),
            ),
            in_specs=[smem] + [vmem] * (6 + len(blocks)),
            out_specs=(vmem, vmem),
            cost_estimate=pl.CostEstimate(
                flops=2 * work * dim * (2 * rows + 2 * half),
                bytes_accessed=work * dim * 2,
                transcendentals=0,
            ),
            name="scan_rows",
        )(base, cand, bias, points, sib, *blocks, sel, near)
        first += sum(counts)

    got = other(sel.astype(jnp.bfloat16))
    flat_blocks = [b for group in groups for b in group]
    counts = (1, 1, 2) * layers
    deep = -(-(half + 1 + rows // dim) // 8) * 8
    work = 2 * chips * rows // 2
    mine, theirs = pl.pallas_call(
        functools.partial(sum_kernel, counts),
        out_shape=(jax.ShapeDtypeStruct((deep, dim), jnp.float32),) * 2,
        in_specs=[vmem] * (3 + len(flat_blocks)),
        out_specs=(vmem, vmem),
        cost_estimate=pl.CostEstimate(
            flops=4 * work * dim * 2 * half,
            bytes_accessed=work * dim * 2,
            transcendentals=work * 2 * half,
        ),
        name="sum_rows",
    )(sel, got, near, *flat_blocks)
    back = other(theirs)
    both = mine + back
    mass = both[half, :half]
    centroids = both[:half] / mass[:, None]
    nearest = jnp.minimum(mine[half + 1 : half + 1 + rows // dim], back[half + 1 : half + 1 + rows // dim])
    point_norm = jnp.sum(points.astype(jnp.float32) ** 2, axis=1)
    return centroids, mass, point_norm + nearest.reshape(rows)


def on_device(chips, cores, points, candidates, owner_slot):
    total = owner_slot.shape[0]
    rows, dim = points.shape
    fits = (
        cores == 2
        and chips in (4, 8, 16)
        and rows % 256 == 0
        and rows % dim == 0
        and dim % LANES == 0
        and total % (32 * chips) == 0
        and total // (2 * chips) <= dim
        and 2 * chips * rows <= LANES * LANES
    )
    if fits:
        return gathered(chips, points, candidates, owner_slot)
    return any_mesh(points, candidates, owner_slot)


def solution(mesh):
    placed = (P(AXES, None), P(), P())
    return jax.shard_map(
        functools.partial(on_device, mesh.shape["dp"], mesh.shape["sub"]),
        mesh=mesh,
        in_specs=placed,
        out_specs=(P(AXES, None), P(AXES), P(AXES)),
        check_vma=False,
    )
```

```python
import functools

import jax
import jax.numpy as jnp
from jax import lax
from jax.experimental import pallas as pl
from jax.experimental.pallas import tpu as pltpu
from jax.sharding import PartitionSpec as P


AXES = ("dp", "sub")
FAR = 3e38
LANES = 128
GRANT = 16 << 20


def pick_rows(round_rows, points, my_device):
    row_count = points.shape[0]
    flat_rows = round_rows.reshape(-1)
    owner_dev = flat_rows // row_count
    local_row = flat_rows % row_count
    mine = owner_dev == my_device
    picked = jnp.where(
        mine[:, None], points[local_row].astype(jnp.float32), jnp.zeros((), jnp.float32)
    )
    return lax.psum(picked, AXES).astype(jnp.bfloat16)


def any_mesh(points, candidates, owner_slot):
    cand = jnp.zeros((owner_slot.shape[0],), jnp.int32).at[owner_slot].set(candidates.reshape(-1))
    chosen = pick_rows(cand, points, lax.axis_index(AXES))
    point_norm = jnp.sum(points.astype(jnp.float32) ** 2, axis=1)
    cand_norm = jnp.sum(chosen.astype(jnp.float32) ** 2, axis=1)
    dots = lax.dot_general(
        points, chosen, (((1,), (1,)), ((), ())), preferred_element_type=jnp.float32
    )
    dist = point_norm[:, None] + cand_norm[None, :] - 2.0 * dots
    nearest = jnp.min(dist, axis=1)
    kernel = jnp.exp(-dist / 0.25).astype(jnp.bfloat16)
    sums = lax.dot_general(
        kernel, points, (((0,), (0,)), ((), ())), preferred_element_type=jnp.float32
    )
    mass = jnp.sum(kernel.astype(jnp.float32), axis=0)
    summed = lax.psum_scatter(sums, AXES, scatter_dimension=0, tiled=True)
    masses = lax.psum_scatter(mass, AXES, scatter_dimension=0, tiled=True)
    return summed / masses[:, None], masses, nearest


def send(x, chips, target):
    pairs = [(d * 2 + c, target(d, c)) for d in range(chips) for c in range(2)]
    return lax.ppermute(x, AXES, pairs)


LAST = (((1,), (1,)), ((), ()))


def column_sums(x):
    square = x * x
    high = square.astype(jnp.bfloat16)
    low = (square - high.astype(jnp.float32)).astype(jnp.bfloat16)
    ones = jnp.ones((8, x.shape[1]), jnp.bfloat16)
    return lax.dot_general(ones, high, LAST, preferred_element_type=jnp.float32) + lax.dot_general(
        ones, low, LAST, preferred_element_type=jnp.float32
    )


def scan_kernel(places, first, base_ref, cand_ref, bias_ref, own_ref, sib_ref, *refs):
    n = len(places)
    block_refs, refs = refs[:n], refs[n:]
    rows, dim = own_ref.shape
    wanted = cand_ref.shape[0]
    if first:
        sel_out, near_out, norm_out = refs
        norm_out[...] = column_sums(own_ref[...].astype(jnp.float32))
        sel = jnp.zeros((wanted, dim), jnp.float32)
        nears = [jnp.full((8, rows), FAR, jnp.float32)] * 2
    else:
        sel_in, near_in, sel_out, near_out = refs
        sel = sel_in[...].astype(jnp.float32)
        nears = [near_in[:, :rows], near_in[:, rows:]]
    lane = lax.broadcasted_iota(jnp.int32, (LANES, LANES), 1)
    spot = lax.broadcasted_iota(jnp.int32, (wanted, rows), 1)
    for place, ref in zip(places, block_refs):
        base = base_ref[place]
        block = ref[...]
        hot = (spot + base == cand_ref[...]).astype(jnp.bfloat16)
        sel += jnp.dot(hot, block, preferred_element_type=jnp.float32)
        cols = []
        for i in range(rows // LANES):
            piece = block[i * LANES : (i + 1) * LANES, :].astype(jnp.float32)
            square = piece * piece
            folded = jnp.where(lane == base // LANES + i, bias_ref[...], 0.0)
            for w in range(dim // LANES):
                folded += square[:, w * LANES : (w + 1) * LANES]
            cols.append(jnp.sum(folded, axis=1, keepdims=True))
        col = jnp.concatenate(cols, axis=0)
        twice = block * jnp.bfloat16(-2.0)
        for h, mine in enumerate((own_ref, sib_ref)):
            dots = lax.dot_general(twice, mine[...], LAST, preferred_element_type=jnp.float32)
            part = jnp.min((dots + col).reshape(rows // 8, 8, rows), axis=0)
            nears[h] = jnp.minimum(nears[h], part)
    sel_out[...] = sel.astype(sel_out.dtype)
    near_out[:, :rows] = nears[0]
    near_out[:, rows:] = nears[1]


def sum_kernel(sel_ref, got_ref, near_ref, *refs):
    block_refs, (mine_ref, theirs_ref) = refs[:-2], refs[-2:]
    wanted, dim = sel_ref.shape
    half = wanted // 2
    rows = near_ref.shape[1] // 2
    got = got_ref[...].astype(jnp.float32)
    chosen32 = sel_ref[...].astype(jnp.float32) + jnp.concatenate([got[half:], got[:half]], axis=0)
    chosen = chosen32.astype(jnp.bfloat16)
    cand_norm = column_sums(chosen32)[:1]
    sums = jnp.zeros((wanted, dim), jnp.float32)
    mass = jnp.zeros((8, wanted), jnp.float32)
    for ref in block_refs:
        block = ref[...]
        wide = block.astype(jnp.float32)
        norm = jnp.sum(wide * wide, axis=1, keepdims=True)
        dots = lax.dot_general(block, chosen, LAST, preferred_element_type=jnp.float32)
        dist = (norm + cand_norm) - 2.0 * dots
        kern = jnp.exp(dist * -4.0).astype(jnp.bfloat16)
        mass += jnp.sum(kern.astype(jnp.float32).reshape(rows // 8, 8, wanted), axis=0)
        sums += lax.dot_general(
            kern, block, (((0,), (0,)), ((), ())), preferred_element_type=jnp.float32
        )
    spare = jnp.zeros((LANES - 8, wanted), jnp.float32)
    mass = jnp.sum(jnp.concatenate([mass, spare], axis=0).T, axis=1, keepdims=True)
    near = jnp.min(near_ref[...], axis=0, keepdims=True)
    for h, ref in enumerate((mine_ref, theirs_ref)):
        ref[:half, :dim] = sums[h * half : (h + 1) * half]
        ref[:half, dim:] = jnp.broadcast_to(mass[h * half : (h + 1) * half], (half, LANES))
        wide = ref.shape[1]
        for w in range(-(-rows // wide)):
            piece = near[:, h * rows + w * wide : h * rows + min(rows, (w + 1) * wide)]
            ref[half + w : half + w + 1, : piece.shape[1]] = piece


def finish_kernel(mine_ref, back_ref, norm_ref, centroids_ref, masses_ref, nearest_ref):
    half, dim = centroids_ref.shape
    rows = nearest_ref.shape[1]
    wide = mine_ref.shape[1]
    mass = mine_ref[:half, dim:] + back_ref[:half, dim:]
    for w in range(dim // LANES):
        at = slice(w * LANES, (w + 1) * LANES)
        centroids_ref[:, at] = (mine_ref[:half, at] + back_ref[:half, at]) / mass
    spare = jnp.zeros((LANES - half, LANES), jnp.float32)
    masses_ref[...] = jnp.concatenate([mass, spare], axis=0).T[:1, :half]
    for w in range(-(-rows // wide)):
        at = slice(w * wide, min(rows, (w + 1) * wide))
        span = at.stop - at.start
        nearest = jnp.minimum(
            mine_ref[half + w : half + w + 1, :span], back_ref[half + w : half + w + 1, :span]
        )
        nearest_ref[:, at] = norm_ref[:1, at] + nearest


SENDS = {
    "sib": (None, "other"),
    "z2": ("own", "two"),
    "z1": ("own", "one"),
    "a0": ("own", "near"),
    "b0": ("own", "far"),
    "e0": ("a0", "far"),
    "a1": ("z1", "near"),
    "b1": ("z1", "far"),
    "e1": ("a1", "far"),
    "z3": ("z2", "one"),
    "a2": ("z2", "near"),
    "b2": ("z2", "far"),
    "e2": ("a2", "far"),
    "a3": ("z3", "near"),
    "b3": ("z3", "far"),
    "e3": ("a3", "far"),
}
ORDER = ("sib", "z2", "z1", "a0", "b0", "s0", "e0", "a1", "b1", "z3", "a2", "b2", "s1", "e1", "s2", "a3", "b3", "s3", "e2", "s4", "e3", "s5", "s6")
SCANS = {
    "s0": ("own",),
    "s1": ("a0", "b0", "z1"),
    "s2": ("e0", "z2"),
    "s3": ("a1", "b1", "e1", "z3"),
    "s4": ("a2", "b2"),
    "s5": ("a3", "b3", "e2"),
    "s6": ("e3",),
}
BLOCKS = sum(SCANS.values(), ())


def gathered(chips, points, candidates, owner_slot):
    rows, dim = points.shape
    total = owner_slot.shape[0]
    half = total // (2 * chips)
    d = lax.axis_index("dp")
    c = lax.axis_index("sub")
    near_bit = jnp.where(c == 0, 1, 2)
    far_bit = 3 - near_bit
    targets = {
        "other": lambda d, c: d * 2 + 1 - c,
        "one": lambda d, c: (d ^ 4) * 2 + c,
        "two": lambda d, c: (d ^ 8) * 2 + c,
        "near": lambda d, c: (d ^ (1 if c == 0 else 2)) * 2 + c,
        "far": lambda d, c: (d ^ (2 if c == 0 else 1)) * 2 + c,
    }
    steps = {"one": 4, "two": 8, "near": near_bit, "far": far_bit}

    flat = candidates.reshape(-1)
    order = jnp.arange(2 * half, dtype=jnp.int32)
    slot = jnp.where(order < half, (2 * d + c) * half + order, (2 * d + 1 - c) * half + order - half)
    cand = jnp.sum(
        jnp.where(owner_slot[None, :] == slot[:, None], flat[None, :], 0), axis=1, keepdims=True
    )
    span = 2 * chips * rows // LANES
    low = (flat[None, :] % LANES == jnp.arange(LANES, dtype=jnp.int32)[:, None]).astype(jnp.bfloat16)
    high = (flat[None, :] // LANES == jnp.arange(span, dtype=jnp.int32)[:, None]).astype(jnp.bfloat16)
    hits = lax.dot_general(low, high, LAST, preferred_element_type=jnp.float32)
    bias = jnp.where(hits > 0, 0.0, FAR).astype(jnp.float32)
    origin = {"own": d}
    for name, (source, way) in SENDS.items():
        if source:
            origin[name] = origin[source] ^ steps[way]
    base = (jnp.stack([origin[name] for name in BLOCKS]) * 2 + c).astype(jnp.int32) * rows

    smem = pl.BlockSpec(memory_space=pltpu.SMEM)
    vmem = pl.BlockSpec(memory_space=pltpu.VMEM)
    grant = pltpu.CompilerParams(vmem_limit_bytes=GRANT)
    sel_shape = jax.ShapeDtypeStruct((2 * half, dim), jnp.bfloat16)
    near_shape = jax.ShapeDtypeStruct((8, 2 * rows), jnp.float32)
    norm_shape = jax.ShapeDtypeStruct((8, rows), jnp.float32)
    blocks = {"own": points}
    sel = near = norm = None
    for name in ORDER:
        if name in SENDS:
            source, way = SENDS[name]
            blocks[name] = send(blocks[source or "own"], chips, targets[way])
            continue
        names = SCANS[name]
        work = len(names) * rows
        first = sel is None
        shapes = (sel_shape, near_shape) + ((norm_shape,) if first else ())
        carried = () if first else (sel, near)
        sel, near, *rest = pl.pallas_call(
            functools.partial(scan_kernel, [BLOCKS.index(b) for b in names], first),
            out_shape=shapes,
            in_specs=[smem] + [vmem] * (4 + len(names) + len(carried)),
            out_specs=(vmem,) * len(shapes),
            cost_estimate=pl.CostEstimate(
                flops=4 * work * dim * (rows + half), bytes_accessed=work * dim, transcendentals=0
            ),
            compiler_params=grant,
            name="scan_rows",
        )(base, cand, bias, points, blocks["sib"], *[blocks[b] for b in names], *carried)
        norm = rest[0] if first else norm

    got = send(sel, chips, targets["other"])
    deep = -(-(half + -(-rows // (dim + LANES))) // 8) * 8
    work = len(BLOCKS) * rows
    mine, theirs = pl.pallas_call(
        sum_kernel,
        out_shape=(jax.ShapeDtypeStruct((deep, dim + LANES), jnp.float32),) * 2,
        in_specs=[vmem] * (3 + len(BLOCKS)),
        out_specs=(vmem, vmem),
        cost_estimate=pl.CostEstimate(
            flops=8 * work * dim * half, bytes_accessed=work * dim * 2, transcendentals=work * 2 * half
        ),
        compiler_params=grant,
        name="sum_rows",
    )(sel, got, near, *[blocks[b] for b in BLOCKS])
    back = send(theirs, chips, targets["other"])
    centroids, masses, nearest = pl.pallas_call(
        finish_kernel,
        out_shape=(
            jax.ShapeDtypeStruct((half, dim), jnp.float32),
            jax.ShapeDtypeStruct((1, half), jnp.float32),
            jax.ShapeDtypeStruct((1, rows), jnp.float32),
        ),
        in_specs=[vmem] * 3,
        out_specs=(vmem,) * 3,
        compiler_params=grant,
        name="finish_rows",
    )(mine, back, norm)
    return centroids, masses.reshape(half), nearest.reshape(rows)


def fits(chips, cores, rows, dim, total):
    return (
        cores == 2
        and chips == 16
        and rows % LANES == 0
        and dim % LANES == 0
        and total % (16 * chips) == 0
        and total // (2 * chips) <= LANES
        and 2 * chips * rows <= LANES * LANES
    )


def on_device(chips, cores, points, candidates, owner_slot):
    if fits(chips, cores, *points.shape, owner_slot.shape[0]):
        return gathered(chips, points, candidates, owner_slot)
    return any_mesh(points, candidates, owner_slot)


def solution(mesh):
    chips, cores = mesh.shape["dp"], mesh.shape["sub"]
    placed = (P(AXES, None), P(), P())
    return jax.shard_map(
        functools.partial(on_device, chips, cores),
        mesh=mesh,
        in_specs=placed,
        out_specs=(P(AXES, None), P(AXES), P(AXES)),
        check_vma=False,
    )
```

```python
import functools
import math

import jax
import jax.numpy as jnp
from jax import lax
from jax.experimental import pallas as pl
from jax.experimental.pallas import tpu as pltpu
from jax.sharding import PartitionSpec as P


AXES = ("dp", "sub")
FAR = 3e38
LANES = 128
SHIFT = 7
GRANT = 16 << 20


def pick_rows(round_rows, points, my_device):
    row_count = points.shape[0]
    flat_rows = round_rows.reshape(-1)
    owner_dev = flat_rows // row_count
    local_row = flat_rows % row_count
    mine = owner_dev == my_device
    picked = jnp.where(
        mine[:, None], points[local_row].astype(jnp.float32), jnp.zeros((), jnp.float32)
    )
    return lax.psum(picked, AXES).astype(jnp.bfloat16)


def any_mesh(points, candidates, owner_slot):
    cand = jnp.zeros((owner_slot.shape[0],), jnp.int32).at[owner_slot].set(candidates.reshape(-1))
    chosen = pick_rows(cand, points, lax.axis_index(AXES))
    point_norm = jnp.sum(points.astype(jnp.float32) ** 2, axis=1)
    cand_norm = jnp.sum(chosen.astype(jnp.float32) ** 2, axis=1)
    dots = lax.dot_general(
        points, chosen, (((1,), (1,)), ((), ())), preferred_element_type=jnp.float32
    )
    dist = point_norm[:, None] + cand_norm[None, :] - 2.0 * dots
    nearest = jnp.min(dist, axis=1)
    kernel = jnp.exp(-dist / 0.25).astype(jnp.bfloat16)
    sums = lax.dot_general(
        kernel, points, (((0,), (0,)), ((), ())), preferred_element_type=jnp.float32
    )
    mass = jnp.sum(kernel.astype(jnp.float32), axis=0)
    summed = lax.psum_scatter(sums, AXES, scatter_dimension=0, tiled=True)
    masses = lax.psum_scatter(mass, AXES, scatter_dimension=0, tiled=True)
    return summed / masses[:, None], masses, nearest


def send(x, chips, target):
    pairs = [(d * 2 + c, target(d, c)) for d in range(chips) for c in range(2)]
    return lax.ppermute(x, AXES, pairs)


LAST = (((1,), (1,)), ((), ()))


def column_sums(x):
    square = x * x
    high = square.astype(jnp.bfloat16)
    low = (square - high.astype(jnp.float32)).astype(jnp.bfloat16)
    ones = jnp.ones((8, x.shape[1]), jnp.bfloat16)
    return lax.dot_general(ones, high, LAST, preferred_element_type=jnp.float32) + lax.dot_general(
        ones, low, LAST, preferred_element_type=jnp.float32
    )


def index_kernel(meta_ref, cand_ref, owner_ref, wanted_ref, bias_ref):
    rounds, width = cand_ref.shape
    total = wanted_ref.shape[0]
    place = lax.broadcasted_iota(jnp.int32, (total, 1), 0)
    half = total // 2
    slot = jnp.where(place < half, meta_ref[0] + place, meta_ref[1] + place - half)
    spot = lax.broadcasted_iota(jnp.int32, (LANES, width), 0)
    wanted = jnp.zeros((total, 1), jnp.float32)
    hits = jnp.zeros((LANES, LANES), jnp.float32)
    for r in range(rounds):
        cand = cand_ref[r : r + 1, :]
        owner = owner_ref[:, r * width : (r + 1) * width]
        found = jnp.where(owner == slot, cand.astype(jnp.float32), 0.0)
        wanted += jnp.sum(found, axis=1, keepdims=True)
        low = ((cand & (LANES - 1)) == spot).astype(jnp.bfloat16)
        high = (lax.shift_right_logical(cand, SHIFT) == spot).astype(jnp.bfloat16)
        hits += lax.dot_general(low, high, LAST, preferred_element_type=jnp.float32)
    wanted_ref[...] = wanted.astype(jnp.int32)
    bias_ref[...] = jnp.where(hits > 0, 0.0, FAR)


def pick_kernel(places, first, base_ref, cand_ref, *refs):
    block_refs, sel_out = refs[: len(places)], refs[-1]
    wanted, dim = sel_out.shape
    sel = jnp.zeros((wanted, dim), jnp.float32) if first else refs[-2][...].astype(jnp.float32)
    for place, ref in zip(places, block_refs):
        spot = lax.broadcasted_iota(jnp.int32, (wanted, ref.shape[0]), 1)
        hot = (spot + base_ref[place] == cand_ref[...]).astype(jnp.bfloat16)
        sel += jnp.dot(hot, ref[...], preferred_element_type=jnp.float32)
    sel_out[...] = sel.astype(sel_out.dtype)


def near_kernel(places, first, base_ref, bias_ref, own_ref, sib_ref, *refs):
    n = len(places)
    block_refs, refs = refs[:n], refs[n:]
    rows, dim = own_ref.shape
    if first:
        near_out, total_out, *norm_outs = refs
        total_out[...] = column_sums(own_ref[...].astype(jnp.float32))
        nears = [jnp.full((8, rows), FAR, jnp.float32)] * 2
    else:
        near_in, near_out, *norm_outs = refs
        nears = [near_in[:, :rows], near_in[:, rows:]]
    lane = lax.broadcasted_iota(jnp.int32, (LANES, LANES), 1)
    for place, ref, norm_out in zip(places, block_refs, norm_outs):
        base = base_ref[place]
        block = ref[...]
        cols = []
        for i in range(rows // LANES):
            piece = block[i * LANES : (i + 1) * LANES, :].astype(jnp.float32)
            square = piece * piece
            folded = square[:, :LANES]
            for w in range(1, dim // LANES):
                folded += square[:, w * LANES : (w + 1) * LANES]
            norm = jnp.sum(folded, axis=1, keepdims=True)
            norm_out[i * LANES : (i + 1) * LANES, :] = jnp.broadcast_to(norm, (LANES, LANES))
            mask = jnp.where(lane == lax.shift_right_logical(base, SHIFT) + i, bias_ref[...], 0.0)
            cols.append(norm + jnp.sum(mask, axis=1, keepdims=True))
        col = jnp.concatenate(cols, axis=0)
        twice = block * jnp.bfloat16(-2.0)
        for h, mine in enumerate((own_ref, sib_ref)):
            dots = lax.dot_general(twice, mine[...], LAST, preferred_element_type=jnp.float32)
            part = jnp.min((dots + col).reshape(rows // 8, 8, rows), axis=0)
            nears[h] = jnp.minimum(nears[h], part)
    near_out[:, :rows] = nears[0]
    near_out[:, rows:] = nears[1]


def both_kernel(places, first, base_ref, cand_ref, bias_ref, own_ref, sib_ref, *refs):
    n = len(places)
    blocks, refs = refs[:n], refs[n:]
    if first:
        sel, near = refs[:1], refs[1:]
    else:
        sel, near = (refs[0], refs[2]), (refs[1], *refs[3:])
    pick_kernel(places, first, base_ref, cand_ref, *blocks, *sel)
    near_kernel(places, first, base_ref, bias_ref, own_ref, sib_ref, *blocks, *near)


def sum_kernel(sel_ref, got_ref, near_ref, *refs):
    n = (len(refs) - 2) // 2
    block_refs, norm_refs, (mine_ref, theirs_ref) = refs[:n], refs[n : 2 * n], refs[2 * n :]
    wanted, dim = sel_ref.shape
    half = wanted // 2
    rows = near_ref.shape[1] // 2
    got = got_ref[...].astype(jnp.float32)
    chosen = sel_ref[...].astype(jnp.float32) + jnp.concatenate([got[half:], got[:half]], axis=0)
    cand_norm = column_sums(chosen)[:1]
    twice = (chosen * -2.0).astype(jnp.bfloat16)
    sums = jnp.zeros((wanted, dim), jnp.float32)
    mass = jnp.zeros((8, wanted), jnp.float32)
    for block_ref, norm_ref in zip(block_refs, norm_refs):
        block = block_ref[...]
        norm = norm_ref[...]
        dots = lax.dot_general(block, twice, LAST, preferred_element_type=jnp.float32)
        dist = jnp.concatenate(
            [
                (norm[:, : min(LANES, wanted - w)] + cand_norm[:, w : w + LANES]) + dots[:, w : w + LANES]
                for w in range(0, wanted, LANES)
            ],
            axis=1,
        )
        kern = jnp.exp2(dist * (-4.0 * math.log2(math.e))).astype(jnp.bfloat16)
        mass += jnp.sum(kern.astype(jnp.float32).reshape(rows // 8, 8, wanted), axis=0)
        sums += lax.dot_general(
            kern, block, (((0,), (0,)), ((), ())), preferred_element_type=jnp.float32
        )
    spare = jnp.zeros((LANES - 8, wanted), jnp.float32)
    mass = jnp.sum(jnp.concatenate([mass, spare], axis=0).T, axis=1, keepdims=True)
    near = jnp.min(near_ref[...], axis=0, keepdims=True)
    for h, ref in enumerate((mine_ref, theirs_ref)):
        ref[:half, :dim] = sums[h * half : (h + 1) * half]
        ref[:half, dim:] = jnp.broadcast_to(mass[h * half : (h + 1) * half], (half, LANES))
        wide = ref.shape[1]
        for w in range(-(-rows // wide)):
            piece = near[:, h * rows + w * wide : h * rows + min(rows, (w + 1) * wide)]
            ref[half + w : half + w + 1, : piece.shape[1]] = piece


def finish_kernel(mine_ref, back_ref, norm_ref, centroids_ref, masses_ref, nearest_ref):
    half, dim = centroids_ref.shape
    rows = nearest_ref.shape[1]
    wide = mine_ref.shape[1]
    mass = mine_ref[:half, dim:] + back_ref[:half, dim:]
    for w in range(dim // LANES):
        at = slice(w * LANES, (w + 1) * LANES)
        centroids_ref[:, at] = (mine_ref[:half, at] + back_ref[:half, at]) / mass
    spare = jnp.zeros((LANES - half, LANES), jnp.float32)
    masses_ref[...] = jnp.concatenate([mass, spare], axis=0).T[:1, :half]
    for w in range(-(-rows // wide)):
        at = slice(w * wide, min(rows, (w + 1) * wide))
        span = at.stop - at.start
        nearest = jnp.minimum(
            mine_ref[half + w : half + w + 1, :span], back_ref[half + w : half + w + 1, :span]
        )
        nearest_ref[:, at] = norm_ref[:1, at] + nearest


SENDS = {
    "sib": ("own", "other"),
    "z1": ("own", "one"),
    "a0": ("own", "near"),
    "z2": ("own", "two"),
    "b0": ("own", "far"),
    "e0": ("a0", "far"),
    "a1": ("z1", "near"),
    "b1": ("z1", "far"),
    "e1": ("e0", "one"),
    "z3": ("z2", "one"),
    "a2": ("z2", "near"),
    "b2": ("z2", "far"),
    "e2": ("z2", "diag"),
    "a3": ("z3", "near"),
    "b3": ("z3", "far"),
    "e3": ("e2", "one"),
    "got": ("sel", "other"),
}
ORDER = ("z1", "a0", "z2", "b0", "sib", "e0", "a1", "b1", "z3", "e2", "a2", "b2", "e1", "s1", "e3", "a3", "b3", "s3", "s5", "p6", "got", "n6")
SCANS = {
    "s1": ("own", "a0", "b0", "z1", "e0"),
    "s3": ("z2", "a1", "b1", "e1", "z3"),
    "s5": ("a2", "b2", "e2", "e3"),
    "p6": ("a3", "b3"),
    "n6": ("a3", "b3"),
}
BLOCKS = sum((names for scan, names in SCANS.items() if scan[0] != "p"), ())


def gathered(chips, points, candidates, owner_slot):
    rows, dim = points.shape
    total = owner_slot.shape[0]
    half = total // (2 * chips)
    d = lax.axis_index("dp")
    c = lax.axis_index("sub")
    near_bit = jnp.where(c == 0, 1, 2)
    far_bit = 3 - near_bit
    targets = {
        "other": lambda d, c: d * 2 + 1 - c,
        "one": lambda d, c: (d ^ 4) * 2 + c,
        "two": lambda d, c: (d ^ 8) * 2 + c,
        "near": lambda d, c: (d ^ (1 if c == 0 else 2)) * 2 + c,
        "far": lambda d, c: (d ^ (2 if c == 0 else 1)) * 2 + c,
        "diag": lambda d, c: (d ^ 3) * 2 + c,
    }
    steps = {"one": 4, "two": 8, "near": near_bit, "far": far_bit, "diag": 3, "other": 0}
    origin = {"own": d, "sel": d}
    for name, (source, way) in SENDS.items():
        origin[name] = origin[source] ^ steps[way]
    base = (jnp.stack([origin[name] for name in BLOCKS]) * 2 + c).astype(jnp.int32) * rows
    meta = (jnp.stack([2 * d + c, 2 * d + 1 - c]) * half).astype(jnp.int32)

    smem = pl.BlockSpec(memory_space=pltpu.SMEM)
    vmem = pl.BlockSpec(memory_space=pltpu.VMEM)
    grant = pltpu.CompilerParams(vmem_limit_bytes=GRANT)
    f32 = jnp.float32
    sel_shape = jax.ShapeDtypeStruct((2 * half, dim), jnp.bfloat16)
    near_shape = jax.ShapeDtypeStruct((8, 2 * rows), f32)
    total_shape = jax.ShapeDtypeStruct((8, rows), f32)
    norm_shape = jax.ShapeDtypeStruct((rows, LANES), f32)

    cand, bias = pl.pallas_call(
        index_kernel,
        out_shape=(
            jax.ShapeDtypeStruct((2 * half, 1), jnp.int32),
            jax.ShapeDtypeStruct((LANES, LANES), f32),
        ),
        in_specs=[smem, vmem, vmem],
        out_specs=(vmem, vmem),
        compiler_params=grant,
        name="index_rows",
    )(meta, candidates, owner_slot.reshape(1, total))

    held = {"own": points}
    norms = {}
    near = own_norm = None
    for name in ORDER:
        if name in SENDS:
            source, way = SENDS[name]
            held[name] = send(held[source], chips, targets[way])
            continue
        names = SCANS[name]
        picks, scans = name[0] != "n", name[0] != "p"
        first = "sel" not in held
        operands = [base] + ([cand] if picks else []) + ([bias, points, held["sib"]] if scans else [])
        operands += [held[b] for b in names]
        if not first:
            operands += ([held["sel"]] if picks else []) + ([near] if scans else [])
        shapes = ([sel_shape] if picks else []) + ([near_shape] if scans else [])
        shapes += ([total_shape] if first else []) + ([norm_shape] * len(names) if scans else [])
        body = {"s": both_kernel, "p": pick_kernel, "n": near_kernel}[name[0]]
        work = len(names) * rows
        out = pl.pallas_call(
            functools.partial(body, [BLOCKS.index(b) for b in names], first),
            out_shape=shapes,
            in_specs=[smem] + [vmem] * (len(operands) - 1),
            out_specs=[vmem] * len(shapes),
            cost_estimate=pl.CostEstimate(
                flops=4 * work * dim * (rows * scans + half * picks),
                bytes_accessed=work * dim,
                transcendentals=0,
            ),
            compiler_params=grant,
            name="scan_rows",
        )(*operands)
        out = list(out)
        if picks:
            held["sel"] = out.pop(0)
        if scans:
            near = out.pop(0)
            if first:
                own_norm = out.pop(0)
            norms.update(zip(names, out))

    deep = -(-(half + -(-rows // (dim + LANES))) // 8) * 8
    work = len(BLOCKS) * rows
    mine, theirs = pl.pallas_call(
        sum_kernel,
        out_shape=(jax.ShapeDtypeStruct((deep, dim + LANES), f32),) * 2,
        in_specs=[vmem] * (3 + 2 * len(BLOCKS)),
        out_specs=(vmem, vmem),
        cost_estimate=pl.CostEstimate(
            flops=8 * work * dim * half, bytes_accessed=work * dim * 2, transcendentals=work * 2 * half
        ),
        compiler_params=grant,
        name="sum_rows",
    )(held["sel"], held["got"], near, *[held[b] for b in BLOCKS], *[norms[b] for b in BLOCKS])
    back = send(theirs, chips, targets["other"])
    centroids, masses, nearest = pl.pallas_call(
        finish_kernel,
        out_shape=(
            jax.ShapeDtypeStruct((half, dim), f32),
            jax.ShapeDtypeStruct((1, half), f32),
            jax.ShapeDtypeStruct((1, rows), f32),
        ),
        in_specs=[vmem] * 3,
        out_specs=(vmem,) * 3,
        compiler_params=grant,
        name="finish_rows",
    )(mine, back, own_norm)
    return centroids, masses.reshape(half), nearest.reshape(rows)


def fits(chips, cores, rows, dim, total):
    return (
        cores == 2
        and chips == 16
        and rows % LANES == 0
        and dim % LANES == 0
        and total % (16 * chips) == 0
        and total // (2 * chips) <= LANES
        and 2 * chips * rows <= LANES * LANES
    )


def on_device(chips, cores, points, candidates, owner_slot):
    if fits(chips, cores, *points.shape, owner_slot.shape[0]):
        return gathered(chips, points, candidates, owner_slot)
    return any_mesh(points, candidates, owner_slot)


def solution(mesh):
    chips, cores = mesh.shape["dp"], mesh.shape["sub"]
    placed = (P(AXES, None), P(), P())
    return jax.shard_map(
        functools.partial(on_device, chips, cores),
        mesh=mesh,
        in_specs=placed,
        out_specs=(P(AXES, None), P(AXES), P(AXES)),
        check_vma=False,
    )
```
